512 devices in a mesh: band: 4 (over x), tile: 16 (over y_lo, z), slab: 8 (over y_hi, core).
Axes of the slice: x: 4, y: 8 (y_hi: 4, y_lo: 2; y = y_hi * 2 + y_lo), z: 8, core: 2. Of those that a mesh axis runs over, the one named last changes fastest.
Arguments:
- strength: float32 [32], P('band'), may hold values from 0.0005 to 0.5
- opacity: float32 [64, 256, 256], P('slab', 'tile'), may hold values from 0.5 to 2
- planck: float32 [64, 256, 256], P('slab', 'tile'), may hold values from 0.5 to 2
- old_populations: float32 [5, 64, 256, 256], P(None, 'slab', 'tile'), may hold values from 0.1 to 1
- line_index: int32 [32], P('band'), may hold values from 0 to 4
- line_weight: float32 [32], P('band'), may hold values from 0.2 to 1
Outputs:
- new_populations: float32 [5, 64, 256, 256], P(None, 'slab', 'tile', 'band')
- new_source: float32 [32, 64, 256, 256], P('band', 'slab', 'tile')
The draws below stay inside these ranges and needn't reach their ends.
Inputs may be any that keep to these rules, and one draw needn't show every extreme that they name: line_index names a transition of the model atom.
All inputs are finite; a program needn't handle non-finite values.
Results may differ from the reference program's by a relative error of at most 0.0001.
Values sent between devices are 32-bit elements; how exact they have to be, the bound alone decides.
No kernel may reach another device: no remote copies, remote signals or barrier semaphores. Data moves between devices by JAX's collectives and lax.ppermute only.
A program may use at most 64 MiB of HBM per device.

```python
import math
import jax
import jax.numpy as jnp
from jax import lax

YCELLS = 256
LINES = 5
LEVELS = 5
NX = 256
NZ = 64
FREQS = 32


def with_ends(result, key, least, largest):
    extent = result.shape
    index_at = [jax.random.randint(jax.random.fold_in(key, axis), (), 0, extent[axis]) for axis in range(len(extent))]
    result = result.at[tuple(index_at)].set(least)
    longest = extent.index(max(extent))
    index_at[longest] = (index_at[longest] + 1) % extent[longest]
    return result.at[tuple(index_at)].set(largest)


def level_of(rng, shape, pieces, smallest, high):
    loudness = 1.0
    for axis_at, shards_of in pieces:
        steps = jax.random.uniform(jax.random.fold_in(jax.random.fold_in(rng, 6), axis_at), (shards_of,), jnp.float32, smallest / len(pieces), high / len(pieces))
        loudness = loudness * jnp.repeat(jnp.exp(steps), shape[axis_at] // shards_of).reshape((-1,) + (1,) * (len(shape) - 1 - axis_at))
    return loudness


def setup_inputs(seed: int = 0) -> dict:
    key_list = jax.random.split(jax.random.key(seed), 7)
    return {
        "strength": jnp.clip(jnp.exp(math.log(0.5) - 6.9077552 * jax.random.uniform(key_list[0], (FREQS,), jnp.float32) ** level_of(key_list[0], (FREQS,), ((0, 4),), -0.2, 0.2)), 0.0005, 0.5),
        "opacity": jnp.clip(jnp.exp(math.log(2.0) - 1.3862944 * jax.random.uniform(key_list[1], (NZ, NX, YCELLS), jnp.float32) ** level_of(key_list[1], (NZ, NX, YCELLS), ((0, 8), (1, 16)), -0.2, 0.2)), 0.5, 2.0),
        "planck": jnp.clip(0.5 + 1.5 * jax.random.uniform(key_list[2], (NZ, NX, YCELLS), jnp.float32) ** level_of(key_list[2], (NZ, NX, YCELLS), ((0, 8), (1, 16)), -0.2, 0.2), 0.5, 2.0),
        "old_populations": jnp.clip(0.1 + 0.9 * jax.random.uniform(key_list[3], (LEVELS, NZ, NX, YCELLS), jnp.float32) ** level_of(key_list[3], (LEVELS, NZ, NX, YCELLS), ((1, 8), (2, 16)), -0.2, 0.2), 0.1, 1.0),
        "line_index": with_ends(jax.random.randint(key_list[4], (FREQS,), 0, LINES), jax.random.fold_in(key_list[4], 1), 0, LINES - 1).astype(jnp.int32),
        "line_weight": jnp.clip(0.2 + 0.8 * jax.random.uniform(key_list[5], (FREQS,), jnp.float32) ** level_of(key_list[5], (FREQS,), ((0, 4),), -0.2, 0.2), 0.2, 1.0),
    }


EPS_THERMAL = 0.1
COLLISION = 0.5
PATH_FACTOR = 1.25
TILT_SHARE = 0.4
LOWER_LEVEL = (0, 0, 1, 1, 2)
UPPER_LEVEL = (3, 4, 3, 4, 4)


def line_sources(levels_now):
    return jnp.stack([levels_now[UPPER_LEVEL[t]] / (levels_now[LOWER_LEVEL[t]] + levels_now[UPPER_LEVEL[t]]) for t in range(5)], axis=0)


def relax(jbar, planck):
    ratios = (jbar + COLLISION * planck[None]) / (1.0 + jbar + COLLISION)
    ground = jnp.ones_like(planck)
    level_three = ratios[0]
    level_four = ratios[1]
    level_one = 0.5 * (level_three / ratios[2] + level_four / ratios[3])
    level_two = level_four / ratios[4]
    stacked = jnp.stack([ground, level_one, level_two, level_three, level_four], axis=0)
    return stacked / jnp.sum(stacked, axis=0)


def reference(strength, opacity, planck, old_populations, line_index, line_weight):
    highest = lax.Precision.HIGHEST
    onehot = (line_index[:, None] == jnp.arange(LINES, dtype=jnp.int32)[None, :]).astype(jnp.float32)
    weighted = onehot * line_weight[:, None] * (LINES / (2.0 * FREQS))
    line_now = jnp.moveaxis(line_sources(old_populations), 1, 0)

    def layer_step(intensity, inputs):
        opacity_now, planck_now, lines_here = inputs
        source_now = EPS_THERMAL * planck_now[None] + (1.0 - EPS_THERMAL) * jnp.einsum("ft,txy->fxy", onehot, lines_here, precision=highest)
        attenuation = jnp.exp(-PATH_FACTOR * strength[:, None, None] * opacity_now[None])[:, None]
        zero_column = jnp.zeros_like(intensity[:, 0, :1])
        from_left = jnp.concatenate([zero_column, intensity[:, 0, :-1]], axis=1)
        from_right = jnp.concatenate([intensity[:, 1, 1:], zero_column], axis=1)
        upwind = jnp.stack([from_left, from_right], axis=1)
        intensity = attenuation * ((1.0 - TILT_SHARE) * intensity + TILT_SHARE * upwind) + (1.0 - attenuation) * source_now[:, None]
        rates_now = jnp.einsum("ft,fxy->txy", weighted, jnp.sum(intensity, axis=1), precision=highest)
        return intensity, rates_now

    start = jnp.zeros((FREQS, 2, NX, YCELLS), jnp.float32)
    _, rates = lax.scan(layer_step, start, (opacity, planck, line_now))
    jbar = jnp.moveaxis(rates, 0, 1)
    new_populations = relax(jbar, planck)
    new_source = EPS_THERMAL * planck[None] + (1.0 - EPS_THERMAL) * jnp.einsum("ft,tzxy->fzxy", onehot, line_sources(new_populations), precision=highest)
    return new_populations, new_source
```

```python
import jax
import jax.numpy as jnp
from jax import lax
from jax.experimental import pallas as pl
from jax.experimental.pallas import tpu as pltpu
from jax.sharding import PartitionSpec as P

LINES = 5
EPS_THERMAL = 0.1
COLLISION = 0.5
PATH_FACTOR = 1.25
TILT_SHARE = 0.4
LOG2E = 1.4426950408889634
LANES = 128
FIELDS = 6
PLANE = ("slab", "tile")


def line_ratios(l1, l2, l3, l4):
    return (
        l3 / (1.0 + l3),
        l4 / (1.0 + l4),
        l3 / (l1 + l3),
        l4 / (l1 + l4),
        l4 / (l2 + l4),
    )


def pack_kernel(band_ref, opacity_ref, planck_ref, levels_ref, out_ref, turned_ref):
    half = pl.multiple_of((band_ref[0] % 2) * 64, 64)
    inverse = 1.0 / levels_ref[0]
    fields = [opacity_ref[...], planck_ref[...]]
    fields += [levels_ref[k] * inverse for k in range(1, 5)]
    for i, field in enumerate(fields):
        turned_ref[i] = field.T
        rows = turned_ref[i, pl.ds(half, 64), :]
        out_ref[pl.ds(i, 64, stride=2 * FIELDS), :] = rows
        out_ref[pl.ds(FIELDS + i, 64, stride=2 * FIELDS), :] = rows


def sweep_kernel(half_ref, in_ref, *refs):
    *param_refs, out_ref, w_ref, v_ref, y_ref, j_ref = refs
    params = param_refs[0][...]
    for ref in param_refs[1:]:
        params = params + ref[...]
    decay = params[0:1] * (-PATH_FACTOR * LOG2E)
    weight = params[1:2]
    line = params[2:3].astype(jnp.int32)
    lane = lax.broadcasted_iota(jnp.int32, (1, LANES), 1)
    lane_tile = (lane // 32) * 4
    row = lax.broadcasted_iota(jnp.int32, (96, LANES), 0)
    row_field, row_tile = row // 16, row % 16
    for c in range(4):
        same = row_tile == lane_tile + c
        for k, want in enumerate((jnp.zeros_like(line), line + 1)):
            hit = jnp.where(same & (row_field == want), 1.0, 0.0).astype(jnp.bfloat16)
            at = c * 256 + k * LANES
            w_ref[0:96, at : at + LANES] = hit
            w_ref[96:192, at : at + LANES] = hit
    row = lax.broadcasted_iota(jnp.int32, (80, LANES), 0)
    row_line, row_tile = row // 16, row % 16
    for c in range(4):
        hit = jnp.where((row_tile == lane_tile + c) & (row_line == line), 1.0, 0.0)
        hit = hit.astype(jnp.bfloat16)
        v_ref[:, c * LANES : (c + 1) * LANES] = hit
        v_ref[:, 512 + c * LANES : 512 + (c + 1) * LANES] = hit

    sub = lax.broadcasted_iota(jnp.int32, (8, LANES), 0)
    first_row, last_row = sub == 0, sub == 7
    lane8 = lax.broadcasted_iota(jnp.int32, (8, LANES), 1)
    inner_left, inner_right = lane8 >= 32, lane8 < 96
    half = half_ref[0]

    def slab(s, state):
        base = s * 96
        op, pk, r1, r2, r3, r4 = [in_ref[pl.ds(base + i, 16, stride=FIELDS), :] for i in range(6)]
        sources = [EPS_THERMAL * pk + (1.0 - EPS_THERMAL) * q for q in line_ratios(r1, r2, r3, r4)]
        parts = jnp.concatenate([op, *sources], axis=0)
        high = parts.astype(jnp.bfloat16)
        low = (parts - high.astype(jnp.float32)).astype(jnp.bfloat16)
        y_ref[...] = lax.dot_general(
            jnp.concatenate([high, low], axis=0),
            w_ref[...],
            (((0,), (0,)), ((), ())),
            preferred_element_type=jnp.float32,
        )
        right, left = list(state[:8]), list(state[8:])
        for z in range(8):
            turned = [pltpu.roll(v, 1, 0) for v in right]
            edge = jnp.where(inner_left, pltpu.roll(turned[7], 32, 1), 0.0)
            up_right = [jnp.where(first_row, turned[p - 1] if p else edge, turned[p]) for p in range(8)]
            turned = [pltpu.roll(v, 7, 0) for v in left]
            edge = jnp.where(inner_right, pltpu.roll(turned[0], 96, 1), 0.0)
            up_left = [jnp.where(last_row, turned[p + 1] if p < 7 else edge, turned[p]) for p in range(8)]
            for c in range(4):
                sums = []
                for k in range(2):
                    p = 2 * c + k
                    rows = slice(z * 16 + k * 8, z * 16 + k * 8 + 8)
                    a = jnp.exp2(y_ref[rows, c * 256 : c * 256 + 128] * decay)
                    b = (1.0 - a) * y_ref[rows, c * 256 + 128 : c * 256 + 256]
                    right[p] = a * ((1.0 - TILT_SHARE) * right[p] + TILT_SHARE * up_right[p]) + b
                    left[p] = a * ((1.0 - TILT_SHARE) * left[p] + TILT_SHARE * up_left[p]) + b
                    sums.append((right[p] + left[p]) * weight)
                both = jnp.concatenate(sums, axis=0)
                high = both.astype(jnp.bfloat16)
                low = (both - high.astype(jnp.float32)).astype(jnp.bfloat16)
                j_ref[z * 16 : z * 16 + 16, c * LANES : (c + 1) * LANES] = high
                j_ref[z * 16 : z * 16 + 16, 512 + c * LANES : 512 + (c + 1) * LANES] = low
        jbar = lax.dot_general(
            v_ref[...], j_ref[...], (((1,), (1,)), ((), ())), preferred_element_type=jnp.float32
        )
        jbar = [jbar[16 * t : 16 * t + 16] for t in range(LINES)]
        ratio = [(j + COLLISION * pk) / (1.0 + j + COLLISION) for j in jbar]
        level_1 = 0.5 * (ratio[0] / ratio[2] + ratio[1] / ratio[3])
        level_2 = ratio[1] / ratio[4]
        out_ref[pl.ds(s * 32, 16, stride=2), :] = jnp.where(half == 0, level_1, ratio[0])
        out_ref[pl.ds(s * 32 + 1, 16, stride=2), :] = jnp.where(half == 0, level_2, ratio[1])
        return tuple(right) + tuple(left)

    lax.fori_loop(0, 8, slab, (jnp.zeros((8, LANES), jnp.float32),) * 16)


def finish_kernel(band_ref, line_ref, in_ref, planck_ref, levels_ref, source_ref, lines_ref):
    l1, l2, l3, l4 = [in_ref[pl.ds(k, 256, stride=4), :].T for k in range(4)]
    for t, q in enumerate(line_ratios(l1, l2, l3, l4)):
        lines_ref[t] = (1.0 - EPS_THERMAL) * q
    thermal = EPS_THERMAL * planck_ref[...]
    for f in range(8):
        source_ref[f] = thermal + lines_ref[line_ref[f]]
    start = band_ref[0] * 256
    own = [in_ref[pl.ds(start + k, 64, stride=4), :] for k in range(4)]
    share = 1.0 / (1.0 + own[0] + own[1] + own[2] + own[3])
    levels_ref[0] = share.T
    for k in range(4):
        levels_ref[k + 1] = (own[k] * share).T


def per_device(strength, opacity, planck, old_populations, line_index, line_weight):
    band = lax.axis_index("band")
    vmem = pl.BlockSpec(memory_space=pltpu.VMEM)
    smem = pl.BlockSpec(memory_space=pltpu.SMEM)
    band_1 = band.astype(jnp.int32).reshape(1)
    half_1 = (lax.axis_index("tile") % 2).astype(jnp.int32).reshape(1)

    own = jnp.stack([strength, line_weight * (LINES / 64.0), line_index.astype(jnp.float32)])
    own = jnp.broadcast_to(own[:, None, None, :], (3, 4, 4, 8))
    mine = (jnp.arange(4) == band)[None, None, :, None]
    own = jnp.where(mine, own, 0.0).reshape(3, LANES)
    own = jnp.concatenate([own, jnp.zeros((5, LANES), jnp.float32)], axis=0)
    params = [own] + [
        lax.ppermute(own, "band", [(i, (i + d) % 4) for i in range(4)]) for d in (1, 2, 3)
    ]

    planck_2d = planck.reshape(128, 256)
    packed = pl.pallas_call(
        pack_kernel,
        grid_spec=pltpu.PrefetchScalarGridSpec(
            num_scalar_prefetch=1,
            grid=(1,),
            in_specs=[
                pl.BlockSpec((128, 128), lambda i, b: (0, b[0] // 2)),
                pl.BlockSpec((128, 128), lambda i, b: (0, b[0] // 2)),
                pl.BlockSpec((5, 128, 128), lambda i, b: (0, 0, b[0] // 2)),
            ],
            out_specs=pl.BlockSpec((128 * FIELDS, LANES), lambda i, b: (0, 0)),
            scratch_shapes=[pltpu.VMEM((FIELDS, 128, 128), jnp.float32)],
        ),
        out_shape=jax.ShapeDtypeStruct((128 * FIELDS, LANES), jnp.float32),
        name="pack",
    )(band_1, opacity.reshape(128, 256), planck_2d, old_populations.reshape(5, 128, 256))

    plane = lax.all_to_all(packed.reshape(128, 3, 2, LANES), PLANE, 0, 0, tiled=True)

    swept = pl.pallas_call(
        sweep_kernel,
        in_specs=[smem, vmem] + [vmem] * len(params),
        out_specs=vmem,
        out_shape=jax.ShapeDtypeStruct((256, LANES), jnp.float32),
        scratch_shapes=[
            pltpu.VMEM((192, 1024), jnp.bfloat16),
            pltpu.VMEM((80, 1024), jnp.bfloat16),
            pltpu.VMEM((128, 1024), jnp.float32),
            pltpu.VMEM((128, 1024), jnp.bfloat16),
        ],
        name="sweep",
    )(half_1, plane.reshape(128 * FIELDS, LANES), *params)

    quarter = lax.all_to_all(swept.reshape(128, 2, LANES), PLANE, 0, 0, tiled=True)
    levels = lax.all_gather(quarter.reshape(256, LANES), "band", axis=0, tiled=True)

    new_levels, new_source = pl.pallas_call(
        finish_kernel,
        in_specs=[smem, smem, vmem, vmem],
        out_specs=[vmem, vmem],
        out_shape=[
            jax.ShapeDtypeStruct((5, 128, 64), jnp.float32),
            jax.ShapeDtypeStruct((8, 128, 256), jnp.float32),
        ],
        scratch_shapes=[pltpu.VMEM((LINES, 128, 256), jnp.float32)],
        name="finish",
    )(band_1, line_index, levels, planck_2d)
    return new_levels.reshape(5, 8, 16, 64), new_source.reshape(8, 8, 16, 256)


def solution(mesh):
    in_specs = (
        P("band"),
        P("slab", "tile", None),
        P("slab", "tile", None),
        P(None, "slab", "tile", None),
        P("band"),
        P("band"),
    )
    out_specs = (P(None, "slab", "tile", "band"), P("band", "slab", "tile", None))
    return jax.shard_map(
        per_device, mesh=mesh, in_specs=in_specs, out_specs=out_specs, check_vma=False
    )
```

```python
import jax
import jax.numpy as jnp
from jax import lax
from jax.experimental import pallas as pl
from jax.experimental.pallas import tpu as pltpu
from jax.sharding import Mesh
from jax.sharding import PartitionSpec as P

LINES = 5
EPS_THERMAL = 0.1
COLLISION = 0.5
PATH_FACTOR = 1.25
TILT_SHARE = 0.4
LOG2E = 1.4426950408889634
LANES = 128
FIELDS = 6
PLANE = ("yhi", "tile")


def line_ratios(l1, l2, l3, l4):
    return (
        l3 / (1.0 + l3),
        l4 / (1.0 + l4),
        l3 / (l1 + l3),
        l4 / (l1 + l4),
        l4 / (l2 + l4),
    )


def pack_kernel(
    band_ref,
    opacity_ref,
    planck_ref,
    levels_ref,
    strength_ref,
    line_ref,
    weight_ref,
    out_ref,
    params_ref,
    turned_ref,
):
    shape = (8, LANES)
    lane = lax.broadcasted_iota(jnp.int32, shape, 1) % 32 - band_ref[0] * 8
    row = lax.broadcasted_iota(jnp.int32, shape, 0)
    own = jnp.zeros(shape, jnp.float32)
    for f in range(8):
        weight = weight_ref[f] * (LINES / 64.0)
        line = line_ref[f].astype(jnp.float32)
        column = jnp.where(row == 0, strength_ref[f], jnp.where(row == 1, weight, jnp.where(row == 2, line, 0.0)))
        own = jnp.where(lane == f, column, own)
    for b in range(4):
        params_ref[b] = own
    half = pl.multiple_of((band_ref[0] % 2) * 64, 64)
    inverse = 1.0 / levels_ref[0]
    fields = [opacity_ref[...], planck_ref[...]]
    fields += [levels_ref[k] * inverse for k in range(1, 5)]
    for i, field in enumerate(fields):
        turned_ref[i] = field.T
        rows = turned_ref[i, pl.ds(half, 64), :]
        out_ref[pl.ds(i, 64, stride=FIELDS), :] = rows


def sweep_kernel(core_ref, in_ref, params_ref, out_ref, w_ref, v_ref, y_ref, j_ref):
    params = params_ref[0] + params_ref[1] + params_ref[2] + params_ref[3]
    decay = params[0:1] * (-PATH_FACTOR * LOG2E)
    weight = params[1:2]
    line = params[2:3].astype(jnp.int32)
    lane = lax.broadcasted_iota(jnp.int32, (1, LANES), 1)
    lane_tile = (lane // 32) * 4
    row = lax.broadcasted_iota(jnp.int32, (96, LANES), 0)
    row_field, row_tile = row // 16, row % 16
    for c in range(4):
        same = row_tile == lane_tile + c
        for k, want in enumerate((jnp.zeros_like(line), line + 1)):
            hit = jnp.where(same & (row_field == want), 1.0, 0.0).astype(jnp.bfloat16)
            at = c * 256 + k * LANES
            w_ref[0:96, at : at + LANES] = hit
            w_ref[96:192, at : at + LANES] = hit
    row = lax.broadcasted_iota(jnp.int32, (80, LANES), 0)
    row_line, row_tile = row // 16, row % 16
    for c in range(4):
        hit = jnp.where((row_tile == lane_tile + c) & (row_line == line), 1.0, 0.0)
        hit = hit.astype(jnp.bfloat16)
        v_ref[:, c * LANES : (c + 1) * LANES] = hit
        v_ref[:, 512 + c * LANES : 512 + (c + 1) * LANES] = hit

    sub = lax.broadcasted_iota(jnp.int32, (8, LANES), 0)
    first_row, last_row = sub == 0, sub == 7
    lane8 = lax.broadcasted_iota(jnp.int32, (8, LANES), 1)
    inner_left, inner_right = lane8 >= 32, lane8 < 96
    core = core_ref[0]

    def slab(s, state, own):
        base = pl.multiple_of((s % 2) * 384 + (s // 2) * 96, 96)
        op, pk, r1, r2, r3, r4 = [in_ref[pl.ds(base + i, 16, stride=FIELDS), :] for i in range(6)]
        sources = [EPS_THERMAL * pk + (1.0 - EPS_THERMAL) * q for q in line_ratios(r1, r2, r3, r4)]
        parts = jnp.concatenate([op, *sources], axis=0)
        high = parts.astype(jnp.bfloat16)
        low = (parts - high.astype(jnp.float32)).astype(jnp.bfloat16)
        y_ref[...] = lax.dot_general(
            jnp.concatenate([high, low], axis=0),
            w_ref[...],
            (((0,), (0,)), ((), ())),
            preferred_element_type=jnp.float32,
        )
        right, left = list(state[:8]), list(state[8:])
        for z in range(8):
            turned = [pltpu.roll(v, 1, 0) for v in right]
            edge = jnp.where(inner_left, pltpu.roll(turned[7], 32, 1), 0.0)
            up_right = [jnp.where(first_row, turned[p - 1] if p else edge, turned[p]) for p in range(8)]
            turned = [pltpu.roll(v, 7, 0) for v in left]
            edge = jnp.where(inner_right, pltpu.roll(turned[0], 96, 1), 0.0)
            up_left = [jnp.where(last_row, turned[p + 1] if p < 7 else edge, turned[p]) for p in range(8)]
            for c in range(4):
                sums = []
                for k in range(2):
                    p = 2 * c + k
                    rows = slice(z * 16 + k * 8, z * 16 + k * 8 + 8)
                    a = jnp.exp2(y_ref[rows, c * 256 : c * 256 + 128] * decay)
                    b = (1.0 - a) * y_ref[rows, c * 256 + 128 : c * 256 + 256]
                    right[p] = a * ((1.0 - TILT_SHARE) * right[p] + TILT_SHARE * up_right[p]) + b
                    left[p] = a * ((1.0 - TILT_SHARE) * left[p] + TILT_SHARE * up_left[p]) + b
                    sums.append((right[p] + left[p]) * weight)
                if own:
                    both = jnp.concatenate(sums, axis=0)
                    high = both.astype(jnp.bfloat16)
                    low = (both - high.astype(jnp.float32)).astype(jnp.bfloat16)
                    j_ref[z * 16 : z * 16 + 16, c * LANES : (c + 1) * LANES] = high
                    j_ref[z * 16 : z * 16 + 16, 512 + c * LANES : 512 + (c + 1) * LANES] = low
        if own:
            jbar = lax.dot_general(
                v_ref[...], j_ref[...], (((1,), (1,)), ((), ())), preferred_element_type=jnp.float32
            )
            jbar = [jbar[16 * t : 16 * t + 16] for t in range(LINES)]
            ratio = [(j + COLLISION * pk) / (1.0 + j + COLLISION) for j in jbar]
            level_1 = 0.5 * (ratio[0] / ratio[2] + ratio[1] / ratio[3])
            level_2 = ratio[1] / ratio[4]
            for k, level in enumerate((level_1, level_2, ratio[0], ratio[1])):
                out_ref[pl.ds((s // 2) * 64 + k, 16, stride=4), :] = level
        return tuple(right) + tuple(left)

    def either(s, state):
        return lax.cond(
            s % 2 == core,
            lambda state: slab(s, state, True),
            lambda state: slab(s, state, False),
            state,
        )

    lax.fori_loop(0, 8, either, (jnp.zeros((8, LANES), jnp.float32),) * 16)


def finish_kernel(band_ref, line_ref, in_ref, planck_ref, levels_ref, source_ref, lines_ref):
    l1, l2, l3, l4 = [in_ref[pl.ds(k, 256, stride=4), :].T for k in range(4)]
    for t, q in enumerate(line_ratios(l1, l2, l3, l4)):
        lines_ref[t] = (1.0 - EPS_THERMAL) * q
    thermal = EPS_THERMAL * planck_ref[...]
    for f in range(8):
        source_ref[f] = thermal + lines_ref[line_ref[f]]
    start = band_ref[0] * 256
    own = [in_ref[pl.ds(start + k, 64, stride=4), :] for k in range(4)]
    share = 1.0 / (1.0 + own[0] + own[1] + own[2] + own[3])
    levels_ref[0] = share.T
    for k in range(4):
        levels_ref[k + 1] = (own[k] * share).T


def per_device(strength, opacity, planck, old_populations, line_index, line_weight):
    band = lax.axis_index("band")
    vmem = pl.BlockSpec(memory_space=pltpu.VMEM)
    smem = pl.BlockSpec(memory_space=pltpu.SMEM)
    band_1 = band.astype(jnp.int32).reshape(1)
    core_1 = lax.axis_index("core").astype(jnp.int32).reshape(1)

    planck_2d = planck.reshape(128, 256)
    packed, own_params = pl.pallas_call(
        pack_kernel,
        grid_spec=pltpu.PrefetchScalarGridSpec(
            num_scalar_prefetch=1,
            grid=(1,),
            in_specs=[
                pl.BlockSpec((128, 128), lambda i, b: (0, b[0] // 2)),
                pl.BlockSpec((128, 128), lambda i, b: (0, b[0] // 2)),
                pl.BlockSpec((5, 128, 128), lambda i, b: (0, 0, b[0] // 2)),
                smem,
                smem,
                smem,
            ],
            out_specs=[
                pl.BlockSpec((64 * FIELDS, LANES), lambda i, b: (0, 0)),
                pl.BlockSpec((4, 8, LANES), lambda i, b: (0, 0, 0)),
            ],
            scratch_shapes=[pltpu.VMEM((FIELDS, 128, 128), jnp.float32)],
        ),
        out_shape=[
            jax.ShapeDtypeStruct((64 * FIELDS, LANES), jnp.float32),
            jax.ShapeDtypeStruct((4, 8, LANES), jnp.float32),
        ],
        name="pack",
    )(
        band_1,
        opacity.reshape(128, 256),
        planck_2d,
        old_populations.reshape(5, 128, 256),
        strength,
        line_index,
        line_weight,
    )

    part = lax.all_to_all(packed.reshape(64, 3, 2, LANES), PLANE, 0, 0, tiled=True)
    params = lax.all_to_all(own_params, "band", 0, 0, tiled=True)
    plane = lax.all_gather(part.reshape(64 * FIELDS, LANES), "core", axis=0, tiled=True)

    swept = pl.pallas_call(
        sweep_kernel,
        in_specs=[smem, vmem, vmem],
        out_specs=vmem,
        out_shape=jax.ShapeDtypeStruct((256, LANES), jnp.float32),
        scratch_shapes=[
            pltpu.VMEM((192, 1024), jnp.bfloat16),
            pltpu.VMEM((80, 1024), jnp.bfloat16),
            pltpu.VMEM((128, 1024), jnp.float32),
            pltpu.VMEM((128, 1024), jnp.bfloat16),
        ],
        compiler_params=pltpu.CompilerParams(vmem_limit_bytes=8 << 20),
        name="sweep",
    )(core_1, plane, params)

    quarter = lax.all_to_all(swept.reshape(64, 4, LANES), PLANE, 0, 0, tiled=True)
    levels = lax.all_gather(quarter.reshape(256, LANES), "band", axis=0, tiled=True)

    new_levels, new_source = pl.pallas_call(
        finish_kernel,
        in_specs=[smem, smem, vmem, vmem],
        out_specs=[vmem, vmem],
        out_shape=[
            jax.ShapeDtypeStruct((5, 128, 64), jnp.float32),
            jax.ShapeDtypeStruct((8, 128, 256), jnp.float32),
        ],
        scratch_shapes=[pltpu.VMEM((LINES, 128, 256), jnp.float32)],
        compiler_params=pltpu.CompilerParams(vmem_limit_bytes=8 << 20),
        name="finish",
    )(band_1, line_index, levels, planck_2d)
    return new_levels.reshape(5, 8, 16, 64), new_source.reshape(8, 8, 16, 256)


def solution(mesh):
    bands, tiles, slabs = (mesh.shape[n] for n in ("band", "tile", "slab"))
    fine = Mesh(mesh.devices.reshape(bands, tiles, slabs // 2, 2), ("band", "tile", "yhi", "core"))
    slab = ("yhi", "core")
    in_specs = (
        P("band"),
        P(slab, "tile", None),
        P(slab, "tile", None),
        P(None, slab, "tile", None),
        P("band"),
        P("band"),
    )
    out_specs = (P(None, slab, "tile", "band"), P("band", slab, "tile", None))
    return jax.shard_map(
        per_device, mesh=fine, in_specs=in_specs, out_specs=out_specs, check_vma=False
    )
```

```python
import jax
import jax.numpy as jnp
from jax import lax
from jax.experimental import pallas as pl
from jax.experimental.pallas import tpu as pltpu
from jax.sharding import Mesh
from jax.sharding import PartitionSpec as P

LINES = 5
EPS_THERMAL = 0.1
COLLISION = 0.5
PATH_FACTOR = 1.25
TILT_SHARE = 0.4
LOG2E = 1.4426950408889634
LANES = 128
FIELDS = 6
PLANE = ("yhi", "tile")


def line_ratios(l1, l2, l3, l4):
    return (
        l3 / (1.0 + l3),
        l4 / (1.0 + l4),
        l3 / (l1 + l3),
        l4 / (l1 + l4),
        l4 / (l2 + l4),
    )


def pack_kernel(
    band_ref,
    opacity_ref,
    planck_ref,
    levels_ref,
    strength_ref,
    line_ref,
    weight_ref,
    out_ref,
    params_ref,
    turned_ref,
):
    shape = (8, LANES)
    lane = lax.broadcasted_iota(jnp.int32, shape, 1) % 32 - band_ref[0] * 8
    row = lax.broadcasted_iota(jnp.int32, shape, 0)
    own = jnp.zeros(shape, jnp.float32)
    for f in range(8):
        weight = weight_ref[f] * (LINES / 64.0)
        line = line_ref[f].astype(jnp.float32)
        column = jnp.where(row == 0, strength_ref[f], jnp.where(row == 1, weight, jnp.where(row == 2, line, 0.0)))
        own = jnp.where(lane == f, column, own)
    params_ref[...] = own
    half = pl.multiple_of((band_ref[0] % 2) * 64, 64)
    inverse = 1.0 / levels_ref[0]
    fields = [opacity_ref[...], planck_ref[...]]
    fields += [levels_ref[k] * inverse for k in range(1, 5)]
    for i, field in enumerate(fields):
        turned_ref[i] = field.T
        rows = turned_ref[i, pl.ds(half, 64), :]
        out_ref[pl.ds(i, 64, stride=FIELDS), :] = rows


def sweep_kernel(core_ref, in_ref, params_ref, out_ref, w_ref, v_ref, even_ref, odd_ref, j_ref):
    params = params_ref[...]
    decay = params[0:1] * (-PATH_FACTOR * LOG2E)
    weight = params[1:2]
    line = params[2:3].astype(jnp.int32)
    lane = lax.broadcasted_iota(jnp.int32, (1, LANES), 1)
    lane_tile = (lane // 32) * 4
    row = lax.broadcasted_iota(jnp.int32, (96, LANES), 0)
    row_field, row_tile = row // 16, row % 16
    for c in range(4):
        same = row_tile == lane_tile + c
        for k, want in enumerate((jnp.zeros_like(line), line + 1)):
            hit = jnp.where(same & (row_field == want), 1.0, 0.0).astype(jnp.bfloat16)
            at = c * 256 + k * LANES
            w_ref[0:96, at : at + LANES] = hit
            w_ref[96:192, at : at + LANES] = hit
    row = lax.broadcasted_iota(jnp.int32, (80, LANES), 0)
    row_line, row_tile = row // 16, row % 16
    for c in range(4):
        hit = jnp.where((row_tile == lane_tile + c) & (row_line == line), 1.0, 0.0)
        hit = hit.astype(jnp.bfloat16)
        v_ref[:, c * LANES : (c + 1) * LANES] = hit
        v_ref[:, 512 + c * LANES : 512 + (c + 1) * LANES] = hit

    sub = lax.broadcasted_iota(jnp.int32, (8, LANES), 0)
    first_row, last_row = sub == 0, sub == 7
    lane8 = lax.broadcasted_iota(jnp.int32, (8, LANES), 1)
    inner_left, inner_right = lane8 >= 32, lane8 < 96
    core = core_ref[0]

    def fields(s):
        base = pl.multiple_of((s % 2) * 384 + (s // 2) * 96, 96)
        return [in_ref[pl.ds(base + i, 16, stride=FIELDS), :] for i in range(6)]

    def spread(s, y_ref):
        op, pk, r1, r2, r3, r4 = fields(s)
        sources = [EPS_THERMAL * pk + (1.0 - EPS_THERMAL) * q for q in line_ratios(r1, r2, r3, r4)]
        parts = jnp.concatenate([op, *sources], axis=0)
        high = parts.astype(jnp.bfloat16)
        low = (parts - high.astype(jnp.float32)).astype(jnp.bfloat16)
        y_ref[...] = lax.dot_general(
            jnp.concatenate([high, low], axis=0),
            w_ref[...],
            (((0,), (0,)), ((), ())),
            preferred_element_type=jnp.float32,
        )

    def slab(s, state, y_ref, own):
        right, left = list(state[:8]), list(state[8:])
        for z in range(8):
            turned = [pltpu.roll(v, 1, 0) for v in right]
            edge = jnp.where(inner_left, pltpu.roll(turned[7], 32, 1), 0.0)
            up_right = [jnp.where(first_row, turned[p - 1] if p else edge, turned[p]) for p in range(8)]
            turned = [pltpu.roll(v, 7, 0) for v in left]
            edge = jnp.where(inner_right, pltpu.roll(turned[0], 96, 1), 0.0)
            up_left = [jnp.where(last_row, turned[p + 1] if p < 7 else edge, turned[p]) for p in range(8)]
            for c in range(4):
                sums = []
                for k in range(2):
                    p = 2 * c + k
                    rows = slice(z * 16 + k * 8, z * 16 + k * 8 + 8)
                    a = jnp.exp2(y_ref[rows, c * 256 : c * 256 + 128] * decay)
                    b = (1.0 - a) * y_ref[rows, c * 256 + 128 : c * 256 + 256]
                    right[p] = a * ((1.0 - TILT_SHARE) * right[p] + TILT_SHARE * up_right[p]) + b
                    left[p] = a * ((1.0 - TILT_SHARE) * left[p] + TILT_SHARE * up_left[p]) + b
                    sums.append((right[p] + left[p]) * weight)
                if own:
                    both = jnp.concatenate(sums, axis=0)
                    high = both.astype(jnp.bfloat16)
                    low = (both - high.astype(jnp.float32)).astype(jnp.bfloat16)
                    j_ref[z * 16 : z * 16 + 16, c * LANES : (c + 1) * LANES] = high
                    j_ref[z * 16 : z * 16 + 16, 512 + c * LANES : 512 + (c + 1) * LANES] = low
        return tuple(right) + tuple(left)

    def relax(s):
        pk = fields(s)[1]
        jbar = lax.dot_general(
            v_ref[...], j_ref[...], (((1,), (1,)), ((), ())), preferred_element_type=jnp.float32
        )
        jbar = [jbar[16 * t : 16 * t + 16] for t in range(LINES)]
        ratio = [(j + COLLISION * pk) / (1.0 + j + COLLISION) for j in jbar]
        level_1 = 0.5 * (ratio[0] / ratio[2] + ratio[1] / ratio[3])
        level_2 = ratio[1] / ratio[4]
        for k, level in enumerate((level_1, level_2, ratio[0], ratio[1])):
            out_ref[pl.ds((s // 2) * 64 + k, 16, stride=4), :] = level

    def sweep_even():
        def two_slabs(i, state):
            spread(2 * i + 1, odd_ref)
            state = slab(2 * i, state, even_ref, True)
            relax(2 * i)
            spread(2 * i + 2, even_ref)
            return slab(2 * i + 1, state, odd_ref, False)

        spread(0, even_ref)
        state = lax.fori_loop(0, 3, two_slabs, start)
        slab(6, state, even_ref, True)
        relax(6)

    def sweep_odd():
        def two_slabs(i, state):
            spread(2 * i + 2, even_ref)
            state = slab(2 * i + 1, state, odd_ref, True)
            relax(2 * i + 1)
            spread(2 * i + 3, odd_ref)
            return slab(2 * i + 2, state, even_ref, False)

        spread(0, even_ref)
        spread(1, odd_ref)
        state = lax.fori_loop(0, 3, two_slabs, slab(0, start, even_ref, False))
        slab(7, state, odd_ref, True)
        relax(7)

    start = (jnp.zeros((8, LANES), jnp.float32),) * 16
    pl.when(core == 0)(sweep_even)
    pl.when(core == 1)(sweep_odd)


def finish_kernel(band_ref, line_ref, in_ref, planck_ref, levels_ref, source_ref, lines_ref):
    l1, l2, l3, l4 = [in_ref[pl.ds(k, 256, stride=4), :].T for k in range(4)]
    for t, q in enumerate(line_ratios(l1, l2, l3, l4)):
        lines_ref[t] = (1.0 - EPS_THERMAL) * q
    thermal = EPS_THERMAL * planck_ref[...]
    for f in range(8):
        source_ref[f] = thermal + lines_ref[line_ref[f]]
    start = band_ref[0] * 256
    own = [in_ref[pl.ds(start + k, 64, stride=4), :] for k in range(4)]
    share = 1.0 / (1.0 + own[0] + own[1] + own[2] + own[3])
    levels_ref[0] = share.T
    for k in range(4):
        levels_ref[k + 1] = (own[k] * share).T


def per_device(strength, opacity, planck, old_populations, line_index, line_weight):
    band = lax.axis_index("band")
    vmem = pl.BlockSpec(memory_space=pltpu.VMEM)
    smem = pl.BlockSpec(memory_space=pltpu.SMEM)
    band_1 = band.astype(jnp.int32).reshape(1)
    core_1 = lax.axis_index("core").astype(jnp.int32).reshape(1)

    planck_2d = planck.reshape(128, 256)
    packed, own_params = pl.pallas_call(
        pack_kernel,
        grid_spec=pltpu.PrefetchScalarGridSpec(
            num_scalar_prefetch=1,
            grid=(1,),
            in_specs=[
                pl.BlockSpec((128, 128), lambda i, b: (0, b[0] // 2)),
                pl.BlockSpec((128, 128), lambda i, b: (0, b[0] // 2)),
                pl.BlockSpec((5, 128, 128), lambda i, b: (0, 0, b[0] // 2)),
                smem,
                smem,
                smem,
            ],
            out_specs=[
                pl.BlockSpec((64 * FIELDS, LANES), lambda i, b: (0, 0)),
                pl.BlockSpec((8, LANES), lambda i, b: (0, 0)),
            ],
            scratch_shapes=[pltpu.VMEM((FIELDS, 128, 128), jnp.float32)],
        ),
        out_shape=[
            jax.ShapeDtypeStruct((64 * FIELDS, LANES), jnp.float32),
            jax.ShapeDtypeStruct((8, LANES), jnp.float32),
        ],
        name="pack",
    )(
        band_1,
        opacity.reshape(128, 256),
        planck_2d,
        old_populations.reshape(5, 128, 256),
        strength,
        line_index,
        line_weight,
    )

    part = lax.all_to_all(packed.reshape(64, 3, 2, LANES), PLANE, 0, 0, tiled=True)
    params = lax.psum(own_params, "band")
    plane = lax.all_gather(part.reshape(64 * FIELDS, LANES), "core", axis=0, tiled=True)

    swept = pl.pallas_call(
        sweep_kernel,
        in_specs=[smem, vmem, vmem],
        out_specs=vmem,
        out_shape=jax.ShapeDtypeStruct((256, LANES), jnp.float32),
        scratch_shapes=[
            pltpu.VMEM((192, 1024), jnp.bfloat16),
            pltpu.VMEM((80, 1024), jnp.bfloat16),
            pltpu.VMEM((128, 1024), jnp.float32),
            pltpu.VMEM((128, 1024), jnp.float32),
            pltpu.VMEM((128, 1024), jnp.bfloat16),
        ],
        compiler_params=pltpu.CompilerParams(vmem_limit_bytes=8 << 20),
        name="sweep",
    )(core_1, plane, params)

    quarter = lax.all_to_all(swept.reshape(64, 4, LANES), PLANE, 0, 0, tiled=True)
    levels = lax.all_gather(quarter.reshape(256, LANES), "band", axis=0, tiled=True)

    new_levels, new_source = pl.pallas_call(
        finish_kernel,
        in_specs=[smem, smem, vmem, vmem],
        out_specs=[vmem, vmem],
        out_shape=[
            jax.ShapeDtypeStruct((5, 128, 64), jnp.float32),
            jax.ShapeDtypeStruct((8, 128, 256), jnp.float32),
        ],
        scratch_shapes=[pltpu.VMEM((LINES, 128, 256), jnp.float32)],
        compiler_params=pltpu.CompilerParams(vmem_limit_bytes=8 << 20),
        name="finish",
    )(band_1, line_index, levels, planck_2d)
    return new_levels.reshape(5, 8, 16, 64), new_source.reshape(8, 8, 16, 256)


def solution(mesh):
    bands, tiles, slabs = (mesh.shape[n] for n in ("band", "tile", "slab"))
    fine = Mesh(mesh.devices.reshape(bands, tiles, slabs // 2, 2), ("band", "tile", "yhi", "core"))
    slab = ("yhi", "core")
    in_specs = (
        P("band"),
        P(slab, "tile", None),
        P(slab, "tile", None),
        P(None, slab, "tile", None),
        P("band"),
        P("band"),
    )
    out_specs = (P(None, slab, "tile", "band"), P("band", slab, "tile", None))
    return jax.shard_map(
        per_device, mesh=fine, in_specs=in_specs, out_specs=out_specs, check_vma=False
    )
```
